32 devices in a mesh: dp: 4 (over x, core), head: 4 (over z), expert: 2 (over y).
Axes of the slice: x: 2, y: 2, z: 4, core: 2. Of those that a mesh axis runs over, the one named last changes fastest.
Arguments:
- tokens: bfloat16 [4, 64, 4096], P('dp', ('head', 'expert')), may hold values from -6 to 6
- cotangent: bfloat16 [4, 64, 4096], P('dp', ('head', 'expert')), may hold values from -1.5 to 1.5
- queries: bfloat16 [4, 64, 32, 128], P('dp', 'expert', 'head'), may hold values from -32 to 32
- key_vectors: bfloat16 [4, 64, 32, 128], P('dp', 'expert', 'head'), may hold values from -32 to 32
- value_routes: int32 [4, 32, 64, 1], P('dp', 'head'), may hold values from 0 to 3; in each aligned block of 8 rows (0 to 7, 8 to 15, ..., all dimensions but the last counted through in order) at most 3 rows name the same one
- output_routes: int32 [4, 32, 64, 1], P('dp', 'head'), may hold values from 0 to 3; in each aligned block of 8 rows (0 to 7, 8 to 15, ..., all dimensions but the last counted through in order) at most 3 rows name the same one
- value_experts: bfloat16 [128, 4096, 128], P(('head', 'expert')), may hold values from -0.09375 to 0.09375
- output_experts: bfloat16 [128, 4096, 128], P(('head', 'expert')), may hold values from -0.09375 to 0.09375
Outputs:
- token_grads: bfloat16 [4, 64, 4096], P('dp', ('head', 'expert'))
- query_grads: bfloat16 [4, 64, 32, 128], P('dp', 'expert', 'head')
- key_grads: bfloat16 [4, 64, 32, 128], P('dp', 'expert', 'head')
- value_grads: bfloat16 [128, 4096, 128], P(('head', 'expert'), 'dp')
- output_grads: bfloat16 [128, 4096, 128], P(('head', 'expert'), 'dp')
The draws below stay inside these ranges and needn't reach their ends.
Inputs may be any that keep to these rules, and one draw needn't show every extreme that they name: value_routes[b, h, t, 0] is the value expert of head h for token t. In each aligned block of 8 tokens of one sequence and head, no expert is chosen more than 3 times, and in every draw some block has exactly 3 for one expert. output_routes[b, h, t, 0] is the output expert of head h for token t. In each aligned block of 8 tokens of one sequence and head, no expert is chosen more than 3 times, and in every draw some block has exactly 3 for one expert.
All inputs are finite; a program needn't handle non-finite values.
Results may differ from the reference program's by a relative error of at most 0.028.
Values may be sent and summed in bfloat16 or wider, within the bound.
A program may use at most 128 MiB of HBM per device.

```python
import math
import jax
import jax.numpy as jnp
import numpy as np
from jax import lax

D = 4096
H = 32
HD = 128
E = 4
TOK_DEV = 8
CAP = 3
SEQ = 64
B = 4


def attention_draw(key):
    folded = jax.random.fold_in(key, 4409)
    subkeys = jax.random.split(folded, 4)
    full_shape = (B, SEQ, H, HD)
    query_raw = jnp.clip(jax.random.normal(subkeys[0], full_shape, jnp.float32), -4.0, 4.0)
    key_raw = jnp.clip(jax.random.normal(subkeys[1], full_shape, jnp.float32), -4.0, 4.0)
    query_scale = jnp.exp(jax.random.uniform(subkeys[2], (B, SEQ, H, 1), jnp.float32, math.log(0.15), math.log(1.5)))
    key_scale = jnp.exp(jax.random.uniform(subkeys[3], (B, SEQ, H, 1), jnp.float32, math.log(0.3), math.log(3.0)))
    query_field = query_raw * query_scale
    key_field = key_raw * key_scale
    return (jnp.clip(query_field, -32.0, 32.0), jnp.clip(key_field, -32.0, 32.0))


def draw_queries(key, part):
    return attention_draw(key)[0].astype(jnp.bfloat16)


def draw_key_vectors(key, part):
    return attention_draw(key)[1].astype(jnp.bfloat16)


def block_scale(own_key, dims, cuts, least, high):
    def one(axis_at, parts):
        steps = jax.random.uniform(jax.random.fold_in(jax.random.fold_in(own_key, 6), axis_at), (parts,), jnp.float32, least / len(cuts), high / len(cuts))
        return jnp.repeat(jnp.exp(steps), dims[axis_at] // parts).reshape((-1,) + (1,) * (len(dims) - axis_at - 1))

    level = one(*cuts[0])
    for cut in cuts[1:]:
        level = level * one(*cut)
    return level


def routed_block(own_key, own, number, rows, count, top, most, skew):
    order = jax.random.permutation(own_key, count)
    crowded, common = shares(count, rows * top, most, skew, True), shares(count, rows * top, most, skew, False)
    places = jnp.arange(count)

    def named(lengths, turn):
        used = int((lengths > 0).sum())
        fixed = max(1, used // 4)
        shifted = fixed + (places - fixed + turn * (used - fixed)) % max(1, count - fixed)
        return jnp.zeros((count,), jnp.int32).at[order[jnp.where(places < fixed, places, shifted)]].set(jnp.asarray(lengths, jnp.int32))

    lengths = jnp.where(number % 4 == 0, named(crowded, number // 4), named(common, number - number // 4 - 1))
    mixed = jax.random.permutation(jax.random.fold_in(own, 3), count)
    giver, sink = mixed[0:count // 2 * 2:2], mixed[1:count // 2 * 2:2]
    room = jnp.minimum(lengths[giver] - 1, most - lengths[sink]) // 2
    room = jnp.where((giver == order[0]) | (sink == order[0]) | (lengths[sink] == 0), 0, jnp.maximum(room, 0))
    shifted = jax.random.randint(jax.random.fold_in(own, 4), (count // 2,), 0, 1 << 20) % (room + 1)
    lengths = lengths.at[giver].add(-shifted).at[sink].add(shifted)
    labels = jnp.searchsorted(jnp.cumsum(lengths), jnp.arange(rows * top), side="right").astype(jnp.int32)
    grid = labels.reshape(top, rows).T
    grid = grid[jax.random.permutation(jax.random.fold_in(own, 1), rows)]
    turn = jax.random.randint(jax.random.fold_in(own, 2), (rows, 1), 0, top)
    return jnp.take_along_axis(grid, (jnp.arange(top)[None, :] + turn) % top, axis=1)


def shares(number_of, total, limit, skew, full):
    portions = [(1 << 20) // math.isqrt(rank ** skew) + 1 for rank in range(1, number_of + 1)]
    largest = limit if full else min(limit, max(-(-total // number_of), total * portions[0] // sum(portions)))
    least = 1 if total - largest >= number_of - 1 else 0
    given, spare = [largest] + [least] * (number_of - 1), total - largest - least * (number_of - 1)
    while spare > 0:
        candidates = [i for i in range(1, number_of) if given[i] < largest] or [i for i in range(1, number_of) if given[i] < limit]
        whole, budget = sum([portions[i] for i in candidates]), spare
        for i in candidates:
            extra = min(limit - given[i], max(1, budget * portions[i] // whole), spare)
            given[i] = given[i] + extra
            spare = spare - extra
    return np.array(given)


def centred(stream_key, shape, width, bound, pieces=(), held_as=jnp.bfloat16):
    gain = block_scale(stream_key, shape, pieces, -0.22, 0.18) if pieces else 1.0
    result = jax.random.normal(stream_key, shape, jnp.float32) * width * gain
    return jnp.minimum(jnp.maximum(result, -bound), bound).astype(held_as)


def setup_inputs(seed: int = 0) -> dict:
    seeds = jax.random.split(jax.random.key(seed), 9)
    tokens = centred(seeds[0], (B, SEQ, D), 1.0, 6.0, ((0, 4), (1, 8)))
    cotangent = centred(seeds[1], (B, SEQ, D), 0.25, 1.5, ((0, 4), (1, 8)))
    queries = draw_queries(jax.random.fold_in(seeds[8], 71), 0)
    key_vectors = draw_key_vectors(jax.random.fold_in(seeds[8], 71), 0)
    value_routes_keys = jax.random.split(jax.random.fold_in(seeds[4], 1), B * H * SEQ // TOK_DEV)
    value_routes_turns = jax.random.permutation(jax.random.fold_in(seeds[4], 3), B * H * SEQ // TOK_DEV)
    value_routes = jax.vmap(lambda own, number: routed_block(jax.random.fold_in(seeds[4], 2), own, number, TOK_DEV, E, 1, CAP, 2))(value_routes_keys, value_routes_turns).reshape((B, H, SEQ, 1))
    output_routes_keys = jax.random.split(jax.random.fold_in(seeds[5], 1), B * H * SEQ // TOK_DEV)
    output_routes_turns = jax.random.permutation(jax.random.fold_in(seeds[5], 3), B * H * SEQ // TOK_DEV)
    output_routes = jax.vmap(lambda own, number: routed_block(jax.random.fold_in(seeds[5], 2), own, number, TOK_DEV, E, 1, CAP, 2))(output_routes_keys, output_routes_turns).reshape((B, H, SEQ, 1))
    value_experts = centred(seeds[6], (H * E, D, HD), D ** -0.5, 0.09375, ((0, 8),))
    output_experts = centred(seeds[7], (H * E, D, HD), D ** -0.5, 0.09375, ((0, 8),))
    return dict(tokens=tokens, cotangent=cotangent, queries=queries, key_vectors=key_vectors, value_routes=value_routes, output_routes=output_routes, value_experts=value_experts, output_experts=output_experts)


def reference(tokens, cotangent, queries, key_vectors, value_routes, output_routes, value_experts, output_experts):
    score_scale = HD ** (-0.5)
    value_weight = value_experts.astype(jnp.float32).reshape(H, E, D, HD)
    output_weight = output_experts.astype(jnp.float32).reshape(H, E, D, HD)
    expert_ids = jnp.arange(E, dtype=jnp.int32)
    positions = jnp.arange(SEQ, dtype=jnp.int32)
    causal = positions[None, :] <= positions[:, None]

    def sequence_step(running, inputs):
        value_sum, output_sum = running
        token_seq, cotangent_seq, query_seq, key_seq, value_seq_routes, output_seq_routes = inputs
        value_pick = (value_seq_routes[:, :, 0, None] == expert_ids).astype(jnp.float32)
        output_pick = (output_seq_routes[:, :, 0, None] == expert_ids).astype(jnp.float32)
        token_float = token_seq.astype(jnp.float32)
        cotangent_float = cotangent_seq.astype(jnp.float32)
        every_value = jnp.einsum('td,hedc->thec', token_float, value_weight)
        values = jnp.einsum('thec,hte->thc', every_value, value_pick).astype(jnp.bfloat16)
        every_upstream = jnp.einsum('td,hedc->thec', cotangent_float, output_weight)
        upstream = jnp.einsum('thec,hte->thc', every_upstream, output_pick).astype(jnp.bfloat16)
        query_float = query_seq.astype(jnp.float32)
        key_float = key_seq.astype(jnp.float32)
        scores = jnp.einsum('ihc,jhc->hij', query_float, key_float) * score_scale
        row_top = jnp.max(jnp.where(causal, scores, -jnp.inf), axis=-1, keepdims=True)
        weights = jnp.where(causal, jnp.exp(scores - row_top), 0.0)
        probs = weights / jnp.sum(weights, axis=-1, keepdims=True)
        prob_half = lax.optimization_barrier(probs.astype(jnp.bfloat16)).astype(jnp.float32)
        value_float = values.astype(jnp.float32)
        upstream_float = upstream.astype(jnp.float32)
        outputs = jnp.einsum('hij,jhc->ihc', prob_half, value_float).astype(jnp.bfloat16)
        output_float = outputs.astype(jnp.float32)
        row_delta = jnp.sum(output_float * upstream_float, axis=-1)
        prob_grads = jnp.einsum('ihc,jhc->hij', upstream_float, value_float)
        score_grads = probs * (prob_grads - row_delta.T[:, :, None])
        score_half = lax.optimization_barrier(score_grads.astype(jnp.bfloat16)).astype(jnp.float32)
        query_grads = (jnp.einsum('hij,jhc->ihc', score_half, key_float) * score_scale).astype(jnp.bfloat16)
        key_grads = (jnp.einsum('hij,ihc->jhc', score_half, query_float) * score_scale).astype(jnp.bfloat16)
        value_half = jnp.einsum('hij,ihc->jhc', prob_half, upstream_float).astype(jnp.bfloat16)
        value_half_float = value_half.astype(jnp.float32)
        value_masked = jnp.transpose(value_pick, (1, 0, 2))[..., None] * value_half_float[:, :, None, :]
        value_term = jnp.einsum('td,thec->hedc', token_float, value_masked).astype(jnp.bfloat16)
        output_masked = jnp.transpose(output_pick, (1, 0, 2))[..., None] * output_float[:, :, None, :]
        output_term = jnp.einsum('td,thec->hedc', cotangent_float, output_masked).astype(jnp.bfloat16)
        value_sum = value_sum + lax.optimization_barrier(value_term).astype(jnp.float32)
        output_sum = output_sum + lax.optimization_barrier(output_term).astype(jnp.float32)

        def head_step(running_sum, head_pos):
            masked = value_pick[head_pos][:, :, None] * value_half_float[:, head_pos][:, None, :]
            head_term = jnp.einsum('tec,edc->td', masked, value_weight[head_pos]).astype(jnp.bfloat16)
            return (running_sum + lax.optimization_barrier(head_term).astype(jnp.float32), None)
        token_total, _ = lax.scan(head_step, jnp.zeros((SEQ, D), jnp.float32), jnp.arange(H, dtype=jnp.int32))
        return ((value_sum, output_sum), (token_total.astype(jnp.bfloat16), query_grads, key_grads))
    zeros = jnp.zeros((H, E, D, HD), jnp.float32)
    sums, stacked = lax.scan(sequence_step, (zeros, zeros), (tokens, cotangent, queries, key_vectors, value_routes, output_routes))
    value_grads = sums[0].reshape(H * E, D, HD).astype(jnp.bfloat16)
    output_grads = sums[1].reshape(H * E, D, HD).astype(jnp.bfloat16)
    return (stacked[0], stacked[1], stacked[2], value_grads, output_grads)
```

```python
import jax
import jax.numpy as jnp
from jax import lax
from jax.sharding import PartitionSpec as P

E = 4
CAP = 3


def slot_rank(routes):
    onehot = (routes[..., None] == jnp.arange(E, dtype=jnp.int32)).astype(jnp.int32)
    before = jnp.cumsum(onehot, axis=-2) - onehot
    return jnp.sum(before * onehot, axis=-1)


def slot_table(routes):
    rank_of = slot_rank(routes)
    expert_hit = routes[..., None, None, :] == jnp.arange(E, dtype=jnp.int32)[:, None, None]
    place_hit = rank_of[..., None, None, :] == jnp.arange(CAP, dtype=jnp.int32)[:, None]
    return jnp.logical_and(expert_hit, place_hit).astype(jnp.bfloat16)


def local(
    tokens,
    cotangent,
    queries,
    key_vectors,
    value_routes,
    output_routes,
    value_experts,
    output_experts,
):
    head_count = lax.axis_size("head")
    expert_count = lax.axis_size("expert")
    sources = head_count * expert_count
    expert_index = lax.axis_index("expert")
    tok_rows = tokens.shape[1]
    model_width = tokens.shape[2]
    query_rows = queries.shape[1]
    groups = queries.shape[2]
    head_dim = queries.shape[3]
    seq_len = value_routes.shape[2]
    pairs_dev = value_experts.shape[0]
    slot_count = sources * CAP
    score_scale = head_dim ** (-0.5)
    value_local = value_routes[0, :, :, 0]
    output_local = output_routes[0, :, :, 0]

    def own_block(route_part):
        shaped = route_part.reshape(groups, head_count, expert_count, tok_rows)
        return lax.dynamic_index_in_dim(shaped, expert_index, 2, keepdims=False)

    own_pair = jnp.stack([own_block(value_local), own_block(output_local)])
    own_routes = lax.all_to_all(own_pair, "head", split_axis=2, concat_axis=1, tiled=True).reshape(
        2, groups * head_count, tok_rows
    )
    value_table = slot_table(own_routes[0]).reshape(
        head_count, expert_count, pairs_dev, CAP, tok_rows
    )

    def pair_rows(route_part, gathered):
        slot_map = slot_table(route_part.reshape(groups, sources, tok_rows))
        slot_map = jnp.moveaxis(slot_map, 2, 1).reshape(groups * E, sources, CAP, tok_rows)
        slot_map = lax.dynamic_slice_in_dim(slot_map, expert_index * pairs_dev, pairs_dev, 0)
        picked = jnp.einsum(
            "psmt,stw->psmw",
            slot_map,
            gathered.reshape(sources, tok_rows, model_width),
            preferred_element_type=jnp.float32,
        )
        return picked.astype(jnp.bfloat16).reshape(pairs_dev, slot_count, model_width)

    whole_tokens, whole_cotangent = (
        lax.all_gather(tokens[0], ("head", "expert"), axis=0, tiled=True),
        lax.all_gather(cotangent[0], ("head", "expert"), axis=0, tiled=True),
    )
    token_slots = pair_rows(value_local, whole_tokens)
    cotangent_slots = pair_rows(output_local, whole_cotangent)
    value_slots = jnp.einsum(
        "prw,pwk->prk", token_slots, value_experts, preferred_element_type=jnp.float32
    ).astype(jnp.bfloat16)
    upstream_slots = jnp.einsum(
        "prw,pwk->prk", cotangent_slots, output_experts, preferred_element_type=jnp.float32
    ).astype(jnp.bfloat16)
    query_start = expert_index * query_rows
    group_values, group_upstream, all_keys = (
        lax.all_gather(value_slots, "expert", axis=0, tiled=True),
        lax.all_gather(upstream_slots, "expert", axis=0, tiled=True),
        lax.all_gather(key_vectors[0], "expert", axis=0, tiled=True),
    )
    token_source = jnp.arange(seq_len, dtype=jnp.int32) // tok_rows
    head_base = jnp.arange(groups, dtype=jnp.int32)[:, None] * E
    value_rank = slot_rank(value_local.reshape(groups, sources, tok_rows)).reshape(groups, seq_len)
    value_index = (head_base + value_local) * slot_count + token_source * CAP + value_rank
    value_rows = group_values.reshape(-1, head_dim)[value_index]
    output_rank = slot_rank(output_local.reshape(groups, sources, tok_rows)).reshape(
        groups, seq_len
    )
    block_routes = lax.dynamic_slice_in_dim(output_local, query_start, query_rows, 1)
    block_rank = lax.dynamic_slice_in_dim(output_rank, query_start, query_rows, 1)
    block_source = lax.dynamic_slice_in_dim(token_source, query_start, query_rows, 0)
    upstream_index = (head_base + block_routes) * slot_count + block_source * CAP + block_rank
    upstream_rows = group_upstream.reshape(-1, head_dim)[upstream_index]
    query_own = queries[0]
    scores = (
        jnp.einsum("ihc,jhc->hij", query_own, all_keys, preferred_element_type=jnp.float32)
        * score_scale
    )
    query_pos = query_start + jnp.arange(query_rows, dtype=jnp.int32)
    causal = jnp.arange(seq_len, dtype=jnp.int32)[None, :] <= query_pos[:, None]
    row_top = jnp.max(jnp.where(causal, scores, -jnp.inf), axis=-1, keepdims=True)
    weights = jnp.where(causal, jnp.exp(scores - row_top), 0.0)
    probs_full = weights / jnp.sum(weights, axis=-1, keepdims=True)
    prob_half = probs_full.astype(jnp.bfloat16)
    outputs = jnp.einsum(
        "hij,hjc->hic", prob_half, value_rows, preferred_element_type=jnp.float32
    ).astype(jnp.bfloat16)
    row_delta = jnp.sum(outputs.astype(jnp.float32) * upstream_rows.astype(jnp.float32), axis=-1)
    prob_grads = jnp.einsum(
        "hic,hjc->hij", upstream_rows, value_rows, preferred_element_type=jnp.float32
    )
    score_grads = (probs_full * (prob_grads - row_delta[:, :, None])).astype(jnp.bfloat16)
    query_grads = (
        jnp.einsum("hij,jhc->ihc", score_grads, all_keys, preferred_element_type=jnp.float32)
        * score_scale
    ).astype(jnp.bfloat16)
    key_part = (
        jnp.einsum("hij,ihc->jhc", score_grads, query_own, preferred_element_type=jnp.float32)
        * score_scale
    )
    value_part = jnp.einsum(
        "hij,hic->jhc", prob_half, upstream_rows, preferred_element_type=jnp.float32
    )
    key_sum, value_sum = (
        lax.psum_scatter(key_part, "expert", scatter_dimension=0, tiled=True),
        lax.psum_scatter(value_part, "expert", scatter_dimension=0, tiled=True),
    )
    value_half = value_sum.astype(jnp.bfloat16)
    block_value_routes = lax.dynamic_slice_in_dim(value_local, query_start, query_rows, 1).reshape(
        groups, head_count, tok_rows
    )
    value_place = slot_table(block_value_routes)
    output_place = slot_table(block_routes.reshape(groups, head_count, tok_rows))
    value_send = jnp.einsum(
        "hsemt,sthc->hesmc",
        value_place,
        value_half.reshape(head_count, tok_rows, groups, head_dim),
        preferred_element_type=jnp.float32,
    )
    value_send = value_send.astype(jnp.bfloat16).reshape(groups * E, head_count * CAP, head_dim)
    output_send = jnp.einsum(
        "hsemt,hstc->hesmc",
        output_place,
        outputs.reshape(groups, head_count, tok_rows, head_dim),
        preferred_element_type=jnp.float32,
    )
    output_send = output_send.astype(jnp.bfloat16).reshape(groups * E, head_count * CAP, head_dim)
    output_slots, grad_slots = (
        lax.all_to_all(output_send, "expert", split_axis=0, concat_axis=1, tiled=True),
        lax.all_to_all(value_send, "expert", split_axis=0, concat_axis=1, tiled=True),
    )
    value_term = jnp.einsum(
        "prw,prk->pwk", token_slots, grad_slots, preferred_element_type=jnp.float32
    )
    output_term = jnp.einsum(
        "prw,prk->pwk", cotangent_slots, output_slots, preferred_element_type=jnp.float32
    )
    value_grads, output_grads = (
        lax.psum_scatter(
            value_term.astype(jnp.bfloat16), "dp", scatter_dimension=1, tiled=True
        ).astype(jnp.float32),
        lax.psum_scatter(
            output_term.astype(jnp.bfloat16), "dp", scatter_dimension=1, tiled=True
        ).astype(jnp.float32),
    )
    token_terms = jnp.einsum(
        "prk,pwk->prw", grad_slots, value_experts, preferred_element_type=jnp.float32
    ).astype(jnp.bfloat16)
    returned = lax.all_to_all(
        token_terms.reshape(pairs_dev, sources, CAP, model_width),
        ("head", "expert"),
        split_axis=1,
        concat_axis=0,
        tiled=True,
    )
    returned = returned.reshape(head_count, expert_count, pairs_dev, CAP, model_width)
    token_grads = jnp.einsum(
        "gjpmt,gjpmw->tw", value_table, returned, preferred_element_type=jnp.float32
    )
    return (
        token_grads.astype(jnp.bfloat16)[None],
        query_grads[None],
        key_sum.astype(jnp.bfloat16)[None],
        value_grads.astype(jnp.bfloat16),
        output_grads.astype(jnp.bfloat16),
    )


def exchanged(
    tokens,
    cotangent,
    queries,
    key_vectors,
    value_routes,
    output_routes,
    value_experts,
    output_experts,
):
    dp_count = lax.axis_size("dp")
    dp_index = lax.axis_index("dp")
    expert_count = lax.axis_size("expert")
    expert_index = lax.axis_index("expert")
    sources = lax.axis_size("head") * expert_count
    tok_rows = tokens.shape[1]
    width = tokens.shape[2] // dp_count
    groups = queries.shape[2]
    head_dim = queries.shape[3]
    seq_len = value_routes.shape[2]
    pairs_dev = value_experts.shape[0]
    own_heads = groups // expert_count
    score_scale = head_dim ** (-0.5)

    rows = jnp.stack([tokens[0], cotangent[0]])
    rows = lax.all_to_all(rows, "dp", split_axis=2, concat_axis=1, tiled=True)
    rows = lax.all_gather(
        rows.reshape(2, dp_count, tok_rows, width), ("head", "expert"), axis=2, tiled=True
    )
    token_rows = rows[0].reshape(dp_count * seq_len, width)
    cotangent_rows = rows[1].reshape(dp_count * seq_len, width)

    routes = jnp.stack([value_routes[0, :, :, 0], output_routes[0, :, :, 0]])
    routes = lax.dynamic_slice_in_dim(routes, expert_index * own_heads, own_heads, 1)
    routes = lax.all_gather(routes, "dp", axis=1)
    picks = jnp.moveaxis(routes, 3, 2)[..., None] == jnp.arange(E, dtype=jnp.int32)
    picks = picks.reshape(2, dp_count * seq_len, own_heads, E, 1)

    pair = jnp.stack([queries[0], key_vectors[0]])
    pair = lax.all_to_all(pair, "expert", split_axis=2, concat_axis=1, tiled=True)
    query_all, key_all = pair[0], pair[1]

    value_weight = lax.dynamic_slice_in_dim(value_experts, dp_index * width, width, 1)
    output_weight = lax.dynamic_slice_in_dim(output_experts, dp_index * width, width, 1)

    def project(source_rows, weight, pick):
        every = jnp.einsum("td,pdk->tpk", source_rows, weight, preferred_element_type=jnp.float32)
        every = every.reshape(dp_count * seq_len, own_heads, E, head_dim)
        return jnp.sum(jnp.where(pick, every, 0.0), axis=2).astype(jnp.bfloat16)

    part = jnp.stack(
        [
            project(token_rows, value_weight, picks[0]).reshape(
                dp_count, seq_len, own_heads, head_dim
            ),
            project(cotangent_rows, output_weight, picks[1]).reshape(
                dp_count, seq_len, own_heads, head_dim
            ),
        ],
        axis=1,
    )
    part = lax.all_to_all(part, "dp", split_axis=0, concat_axis=0, tiled=True)
    whole = jnp.sum(part.astype(jnp.float32), axis=0).astype(jnp.bfloat16)
    values, upstream = whole[0], whole[1]

    scores = (
        jnp.einsum("ihc,jhc->hij", query_all, key_all, preferred_element_type=jnp.float32)
        * score_scale
    )
    position = jnp.arange(seq_len, dtype=jnp.int32)
    causal = position[None, :] <= position[:, None]
    row_top = jnp.max(jnp.where(causal, scores, -jnp.inf), axis=-1, keepdims=True)
    weights = jnp.where(causal, jnp.exp(scores - row_top), 0.0)
    probs = weights / jnp.sum(weights, axis=-1, keepdims=True)
    prob_half = probs.astype(jnp.bfloat16)
    outputs = jnp.einsum(
        "hij,jhc->ihc", prob_half, values, preferred_element_type=jnp.float32
    ).astype(jnp.bfloat16)
    row_delta = jnp.sum(outputs.astype(jnp.float32) * upstream.astype(jnp.float32), axis=-1)
    prob_grads = jnp.einsum("ihc,jhc->hij", upstream, values, preferred_element_type=jnp.float32)
    value_half = jnp.einsum(
        "hij,ihc->jhc", prob_half, upstream, preferred_element_type=jnp.float32
    ).astype(jnp.bfloat16)
    score_grads = (probs * (prob_grads - row_delta.T[:, :, None])).astype(jnp.bfloat16)
    query_grads = (
        jnp.einsum("hij,jhc->ihc", score_grads, key_all, preferred_element_type=jnp.float32)
        * score_scale
    ).astype(jnp.bfloat16)
    key_grads = (
        jnp.einsum("hij,ihc->jhc", score_grads, query_all, preferred_element_type=jnp.float32)
        * score_scale
    ).astype(jnp.bfloat16)

    factors = lax.all_gather(jnp.stack([value_half, outputs]), "dp", axis=1)
    factors = factors.reshape(2, dp_count * seq_len, own_heads, 1, head_dim)
    factors = jnp.where(picks, factors, jnp.zeros((), jnp.bfloat16)).reshape(
        2, dp_count * seq_len, pairs_dev, head_dim
    )
    token_part = jnp.einsum(
        "tpk,pdk->td", factors[0], value_weight, preferred_element_type=jnp.float32
    ).astype(jnp.bfloat16)
    token_part = lax.all_to_all(
        token_part.reshape(dp_count * sources, tok_rows, width),
        ("dp", "head", "expert"),
        split_axis=0,
        concat_axis=0,
        tiled=True,
    )
    token_grads = jnp.sum(
        token_part.reshape(dp_count, sources, tok_rows, width).astype(jnp.float32), axis=1
    ).astype(jnp.bfloat16)
    token_grads = jnp.moveaxis(token_grads, 0, 1).reshape(tok_rows, dp_count * width)
    value_grads = jnp.einsum(
        "td,tpk->pdk", token_rows, factors[0], preferred_element_type=jnp.float32
    ).astype(jnp.bfloat16)
    output_grads = jnp.einsum(
        "td,tpk->pdk", cotangent_rows, factors[1], preferred_element_type=jnp.float32
    ).astype(jnp.bfloat16)
    back = lax.all_to_all(
        jnp.stack([query_grads, key_grads]), "expert", split_axis=1, concat_axis=2, tiled=True
    )
    return token_grads[None], back[0][None], back[1][None], value_grads, output_grads


def chosen(*args):
    groups, pairs_dev = args[2].shape[2], args[6].shape[0]
    expert_count = lax.axis_size("expert")
    whole_heads = groups % expert_count == 0 and pairs_dev == groups // expert_count * E
    if whole_heads and args[0].shape[2] % (lax.axis_size("dp") * 128) == 0:
        return exchanged(*args)
    return local(*args)


def solution(mesh):
    return jax.shard_map(
        chosen,
        mesh=mesh,
        in_specs=(
            P("dp", ("head", "expert"), None),
            P("dp", ("head", "expert"), None),
            P("dp", "expert", "head", None),
            P("dp", "expert", "head", None),
            P("dp", "head", None, None),
            P("dp", "head", None, None),
            P(("head", "expert"), None, None),
            P(("head", "expert"), None, None),
        ),
        out_specs=(
            P("dp", ("head", "expert"), None),
            P("dp", "expert", "head", None),
            P("dp", "expert", "head", None),
            P(("head", "expert"), "dp", None),
            P(("head", "expert"), "dp", None),
        ),
        check_vma=False,
    )
```

```python
import functools

import jax
import jax.numpy as jnp
from jax import lax
from jax.experimental import pallas as pl
from jax.experimental.pallas import tpu as pltpu
from jax.sharding import PartitionSpec as P

E = 4
CAP = 3


def slot_rank(routes):
    onehot = (routes[..., None] == jnp.arange(E, dtype=jnp.int32)).astype(jnp.int32)
    before = jnp.cumsum(onehot, axis=-2) - onehot
    return jnp.sum(before * onehot, axis=-1)


def slot_table(routes):
    rank_of = slot_rank(routes)
    expert_hit = routes[..., None, None, :] == jnp.arange(E, dtype=jnp.int32)[:, None, None]
    place_hit = rank_of[..., None, None, :] == jnp.arange(CAP, dtype=jnp.int32)[:, None]
    return jnp.logical_and(expert_hit, place_hit).astype(jnp.bfloat16)


def local(
    tokens,
    cotangent,
    queries,
    key_vectors,
    value_routes,
    output_routes,
    value_experts,
    output_experts,
):
    head_count = lax.axis_size("head")
    expert_count = lax.axis_size("expert")
    sources = head_count * expert_count
    expert_index = lax.axis_index("expert")
    tok_rows = tokens.shape[1]
    model_width = tokens.shape[2]
    query_rows = queries.shape[1]
    groups = queries.shape[2]
    head_dim = queries.shape[3]
    seq_len = value_routes.shape[2]
    pairs_dev = value_experts.shape[0]
    slot_count = sources * CAP
    score_scale = head_dim ** (-0.5)
    value_local = value_routes[0, :, :, 0]
    output_local = output_routes[0, :, :, 0]

    def own_block(route_part):
        shaped = route_part.reshape(groups, head_count, expert_count, tok_rows)
        return lax.dynamic_index_in_dim(shaped, expert_index, 2, keepdims=False)

    own_pair = jnp.stack([own_block(value_local), own_block(output_local)])
    own_routes = lax.all_to_all(own_pair, "head", split_axis=2, concat_axis=1, tiled=True).reshape(
        2, groups * head_count, tok_rows
    )
    value_table = slot_table(own_routes[0]).reshape(
        head_count, expert_count, pairs_dev, CAP, tok_rows
    )

    def pair_rows(route_part, gathered):
        slot_map = slot_table(route_part.reshape(groups, sources, tok_rows))
        slot_map = jnp.moveaxis(slot_map, 2, 1).reshape(groups * E, sources, CAP, tok_rows)
        slot_map = lax.dynamic_slice_in_dim(slot_map, expert_index * pairs_dev, pairs_dev, 0)
        picked = jnp.einsum(
            "psmt,stw->psmw",
            slot_map,
            gathered.reshape(sources, tok_rows, model_width),
            preferred_element_type=jnp.float32,
        )
        return picked.astype(jnp.bfloat16).reshape(pairs_dev, slot_count, model_width)

    whole_tokens, whole_cotangent = (
        lax.all_gather(tokens[0], ("head", "expert"), axis=0, tiled=True),
        lax.all_gather(cotangent[0], ("head", "expert"), axis=0, tiled=True),
    )
    token_slots = pair_rows(value_local, whole_tokens)
    cotangent_slots = pair_rows(output_local, whole_cotangent)
    value_slots = jnp.einsum(
        "prw,pwk->prk", token_slots, value_experts, preferred_element_type=jnp.float32
    ).astype(jnp.bfloat16)
    upstream_slots = jnp.einsum(
        "prw,pwk->prk", cotangent_slots, output_experts, preferred_element_type=jnp.float32
    ).astype(jnp.bfloat16)
    query_start = expert_index * query_rows
    group_values, group_upstream, all_keys = (
        lax.all_gather(value_slots, "expert", axis=0, tiled=True),
        lax.all_gather(upstream_slots, "expert", axis=0, tiled=True),
        lax.all_gather(key_vectors[0], "expert", axis=0, tiled=True),
    )
    token_source = jnp.arange(seq_len, dtype=jnp.int32) // tok_rows
    head_base = jnp.arange(groups, dtype=jnp.int32)[:, None] * E
    value_rank = slot_rank(value_local.reshape(groups, sources, tok_rows)).reshape(groups, seq_len)
    value_index = (head_base + value_local) * slot_count + token_source * CAP + value_rank
    value_rows = group_values.reshape(-1, head_dim)[value_index]
    output_rank = slot_rank(output_local.reshape(groups, sources, tok_rows)).reshape(
        groups, seq_len
    )
    block_routes = lax.dynamic_slice_in_dim(output_local, query_start, query_rows, 1)
    block_rank = lax.dynamic_slice_in_dim(output_rank, query_start, query_rows, 1)
    block_source = lax.dynamic_slice_in_dim(token_source, query_start, query_rows, 0)
    upstream_index = (head_base + block_routes) * slot_count + block_source * CAP + block_rank
    upstream_rows = group_upstream.reshape(-1, head_dim)[upstream_index]
    query_own = queries[0]
    scores = (
        jnp.einsum("ihc,jhc->hij", query_own, all_keys, preferred_element_type=jnp.float32)
        * score_scale
    )
    query_pos = query_start + jnp.arange(query_rows, dtype=jnp.int32)
    causal = jnp.arange(seq_len, dtype=jnp.int32)[None, :] <= query_pos[:, None]
    row_top = jnp.max(jnp.where(causal, scores, -jnp.inf), axis=-1, keepdims=True)
    weights = jnp.where(causal, jnp.exp(scores - row_top), 0.0)
    probs_full = weights / jnp.sum(weights, axis=-1, keepdims=True)
    prob_half = probs_full.astype(jnp.bfloat16)
    outputs = jnp.einsum(
        "hij,hjc->hic", prob_half, value_rows, preferred_element_type=jnp.float32
    ).astype(jnp.bfloat16)
    row_delta = jnp.sum(outputs.astype(jnp.float32) * upstream_rows.astype(jnp.float32), axis=-1)
    prob_grads = jnp.einsum(
        "hic,hjc->hij", upstream_rows, value_rows, preferred_element_type=jnp.float32
    )
    score_grads = (probs_full * (prob_grads - row_delta[:, :, None])).astype(jnp.bfloat16)
    query_grads = (
        jnp.einsum("hij,jhc->ihc", score_grads, all_keys, preferred_element_type=jnp.float32)
        * score_scale
    ).astype(jnp.bfloat16)
    key_part = (
        jnp.einsum("hij,ihc->jhc", score_grads, query_own, preferred_element_type=jnp.float32)
        * score_scale
    )
    value_part = jnp.einsum(
        "hij,hic->jhc", prob_half, upstream_rows, preferred_element_type=jnp.float32
    )
    key_sum, value_sum = (
        lax.psum_scatter(key_part, "expert", scatter_dimension=0, tiled=True),
        lax.psum_scatter(value_part, "expert", scatter_dimension=0, tiled=True),
    )
    value_half = value_sum.astype(jnp.bfloat16)
    block_value_routes = lax.dynamic_slice_in_dim(value_local, query_start, query_rows, 1).reshape(
        groups, head_count, tok_rows
    )
    value_place = slot_table(block_value_routes)
    output_place = slot_table(block_routes.reshape(groups, head_count, tok_rows))
    value_send = jnp.einsum(
        "hsemt,sthc->hesmc",
        value_place,
        value_half.reshape(head_count, tok_rows, groups, head_dim),
        preferred_element_type=jnp.float32,
    )
    value_send = value_send.astype(jnp.bfloat16).reshape(groups * E, head_count * CAP, head_dim)
    output_send = jnp.einsum(
        "hsemt,hstc->hesmc",
        output_place,
        outputs.reshape(groups, head_count, tok_rows, head_dim),
        preferred_element_type=jnp.float32,
    )
    output_send = output_send.astype(jnp.bfloat16).reshape(groups * E, head_count * CAP, head_dim)
    output_slots, grad_slots = (
        lax.all_to_all(output_send, "expert", split_axis=0, concat_axis=1, tiled=True),
        lax.all_to_all(value_send, "expert", split_axis=0, concat_axis=1, tiled=True),
    )
    value_term = jnp.einsum(
        "prw,prk->pwk", token_slots, grad_slots, preferred_element_type=jnp.float32
    )
    output_term = jnp.einsum(
        "prw,prk->pwk", cotangent_slots, output_slots, preferred_element_type=jnp.float32
    )
    value_grads, output_grads = (
        lax.psum_scatter(
            value_term.astype(jnp.bfloat16), "dp", scatter_dimension=1, tiled=True
        ).astype(jnp.float32),
        lax.psum_scatter(
            output_term.astype(jnp.bfloat16), "dp", scatter_dimension=1, tiled=True
        ).astype(jnp.float32),
    )
    token_terms = jnp.einsum(
        "prk,pwk->prw", grad_slots, value_experts, preferred_element_type=jnp.float32
    ).astype(jnp.bfloat16)
    returned = lax.all_to_all(
        token_terms.reshape(pairs_dev, sources, CAP, model_width),
        ("head", "expert"),
        split_axis=1,
        concat_axis=0,
        tiled=True,
    )
    returned = returned.reshape(head_count, expert_count, pairs_dev, CAP, model_width)
    token_grads = jnp.einsum(
        "gjpmt,gjpmw->tw", value_table, returned, preferred_element_type=jnp.float32
    )
    return (
        token_grads.astype(jnp.bfloat16)[None],
        query_grads[None],
        key_sum.astype(jnp.bfloat16)[None],
        value_grads.astype(jnp.bfloat16),
        output_grads.astype(jnp.bfloat16),
    )


def fused_kernel(
    sizes,
    tok,
    cot,
    q_in,
    k_in,
    routes_in,
    value_hbm,
    output_hbm,
    tok_out,
    qg_out,
    kg_out,
    vg_out,
    og_out,
    rows,
    flat,
    flat_t,
    routes,
    weight,
    heads_in,
    part,
    part_in,
    factor,
    masked,
    score_keep,
    back,
    back_in,
    term,
    term_in,
    grads,
    sem_weight,
    sem_own,
    sem_rows,
    sem_routes,
    sem_line,
    sem_side,
    sem_heads,
    sem_part,
    sem_factor,
    sem_back,
    sem_term,
    sem_grads,
):
    dn, gn, jn, own_heads, query_rows, tok_rows, width, head_dim = sizes
    sources = gn * jn
    seq_len = sources * tok_rows
    scale = head_dim ** (-0.5)
    d, g, j = lax.axis_index("dp"), lax.axis_index("head"), lax.axis_index("expert")
    block = g * jn + j
    f32, bf16 = jnp.float32, jnp.bfloat16

    def at(dd, gg, jj):
        return {"dp": lax.rem(d + dd, dn), "head": lax.rem(g + gg, gn), "expert": lax.rem(j + jj, jn)}

    others = [
        (dd, gg, jj)
        for dd in range(dn)
        for gg in range(gn)
        for jj in range(jn)
        if (dd, gg, jj) != (0, 0, 0)
    ]
    sent = []

    def send(src, dst, sems, slot, where):
        copy = pltpu.make_async_remote_copy(
            src_ref=src,
            dst_ref=dst,
            send_sem=sems.at[(0,) + slot],
            recv_sem=sems.at[(1,) + slot],
            device_id=at(*where),
            device_id_type=pl.DeviceIdType.MESH,
        )
        copy.start()
        sent.append(copy)
        return copy

    def columns(index):
        return pl.ds(pl.multiple_of(index * width, 128), width)

    weights_on_way = [
        pltpu.make_async_copy(hbm.at[:, columns(d), :], weight.at[i], sem_weight.at[i])
        for i, hbm in enumerate((value_hbm, output_hbm))
    ]
    for copy in weights_on_way:
        copy.start()
    own = [
        pltpu.make_async_copy(tok.at[:, columns(d)], rows.at[block, 0, d], sem_own.at[0]),
        pltpu.make_async_copy(cot.at[:, columns(d)], rows.at[block, 1, d], sem_own.at[1]),
        pltpu.make_async_copy(routes_in, routes.at[d], sem_own.at[2]),
        pltpu.make_async_copy(q_in.at[j], heads_in.at[0, j], sem_own.at[3]),
        pltpu.make_async_copy(k_in.at[j], heads_in.at[1, j], sem_own.at[4]),
    ]
    for copy in own:
        copy.start()

    barrier = pltpu.get_barrier_semaphore()
    for where in others:
        pl.semaphore_signal(
            barrier, inc=1, device_id=at(*where), device_id_type=pl.DeviceIdType.MESH
        )
    pl.semaphore_wait(barrier, len(others))

    first = []
    for dd in range(1, dn):
        target = columns(lax.rem(d + dd, dn))
        first.append(send(tok.at[:, target], rows.at[block, 0, d], sem_rows, (dd, 0), (dd, 0, 0)))
        first.append(send(cot.at[:, target], rows.at[block, 1, d], sem_rows, (dd, 1), (dd, 0, 0)))
    for copy in own:
        copy.wait()
    for copy in first:
        copy.wait_recv()
    line = [
        send(rows.at[block], rows.at[block], sem_line, (gg,), (0, gg, 0)) for gg in range(1, gn)
    ]
    side = [
        send(rows.at[block], rows.at[block], sem_side, (0, jj), (0, 0, jj)) for jj in range(1, jn)
    ]
    late = [
        send(routes_in, routes.at[d], sem_routes, (dd,), (dd, 0, 0)) for dd in range(1, dn)
    ]
    for jj in range(1, jn):
        peer = lax.rem(j + jj, jn)
        late.append(send(q_in.at[peer], heads_in.at[0, j], sem_heads, (0, jj), (0, 0, jj)))
        late.append(send(k_in.at[peer], heads_in.at[1, j], sem_heads, (1, jj), (0, 0, jj)))
    for gg in range(1, gn):
        line[gg - 1].wait_recv()
        came = lax.rem(g + gn - gg, gn) * jn + j
        for jj in range(1, jn):
            side.append(send(rows.at[came], rows.at[came], sem_side, (gg, jj), (0, 0, jj)))
    for copy in side + late:
        copy.wait_recv()

    for i in range(2):
        for b in range(dn):
            piece = jnp.concatenate([rows[s, i, b].astype(f32) for s in range(sources)], axis=0)
            flat[i, b * seq_len : (b + 1) * seq_len, :] = piece.astype(bf16)
    for copy in weights_on_way:
        copy.wait()

    def column(i, h, b):
        c = i * own_heads + h
        return jnp.broadcast_to(routes[b, :, c : c + 1], (seq_len, head_dim))

    for i in range(2):
        for h in range(own_heads):
            picked = [jnp.zeros((seq_len, head_dim), f32) for _ in range(dn)]
            for e in range(0, E, 2):
                p = h * E + e
                both = jnp.concatenate([weight[i, p], weight[i, p + 1]], axis=1)
                every = jnp.dot(flat[i], both, preferred_element_type=f32)
                for b in range(dn):
                    own_rows = every[b * seq_len : (b + 1) * seq_len]
                    route = column(i, h, b)
                    picked[b] = jnp.where(route == e, own_rows[:, :head_dim], picked[b])
                    picked[b] = jnp.where(route == e + 1, own_rows[:, head_dim:], picked[b])
            for b in range(dn):
                part[b, i, h] = picked[b].astype(bf16)
    summed = [
        send(part.at[lax.rem(d + dd, dn)], part_in.at[dd], sem_part, (dd,), (dd, 0, 0))
        for dd in range(1, dn)
    ]
    for i in range(2):
        flat_t[i] = flat[i].T
    for copy in summed:
        copy.wait_recv()

    query_pos = lax.broadcasted_iota(jnp.int32, (seq_len, seq_len), 0)
    key_pos = lax.broadcasted_iota(jnp.int32, (seq_len, seq_len), 1)
    causal = key_pos <= query_pos

    def joined(i, h):
        return jnp.concatenate([heads_in[i, jj, h] for jj in range(jn)], axis=0)

    def total(i, h):
        whole = part[d, i, h].astype(f32)
        for dd in range(1, dn):
            whole = whole + part_in[dd, i, h].astype(f32)
        return whole.astype(bf16)

    def across(a, b):
        return lax.dot_general(a, b, (((1,), (1,)), ((), ())), preferred_element_type=f32)

    def over_rows(a, b):
        return lax.dot_general(a, b, (((0,), (0,)), ((), ())), preferred_element_type=f32)

    for h in range(own_heads):
        query, key = joined(0, h), joined(1, h)
        value, upstream = total(0, h), total(1, h)
        scores = across(query, key) * scale
        top = jnp.max(jnp.where(causal, scores, -jnp.inf), axis=-1, keepdims=True)
        soft = jnp.where(causal, jnp.exp(scores - top), 0.0)
        probs = soft / jnp.sum(soft, axis=-1, keepdims=True)
        half = probs.astype(bf16)
        output = jnp.dot(half, value, preferred_element_type=f32).astype(bf16)
        factor[d, 0, h] = over_rows(half, upstream).astype(bf16)
        factor[d, 1, h] = output
        delta = jnp.sum(output.astype(f32) * upstream.astype(f32), axis=-1, keepdims=True)
        score_keep[h] = (probs * (across(upstream, value) - delta)).astype(bf16)
    spread = [
        send(factor.at[d], factor.at[d], sem_factor, (dd,), (dd, 0, 0)) for dd in range(1, dn)
    ]
    for h in range(own_heads):
        query, key, score = joined(0, h), joined(1, h), score_keep[h]
        query_grad = (jnp.dot(score, key, preferred_element_type=f32) * scale).astype(bf16)
        key_grad = (over_rows(score, query) * scale).astype(bf16)
        for jj in range(jn):
            back[jj, 0, h] = query_grad[jj * query_rows : (jj + 1) * query_rows]
            back[jj, 1, h] = key_grad[jj * query_rows : (jj + 1) * query_rows]
    returned = [
        send(back.at[lax.rem(j + jj, jn)], back_in.at[j], sem_back, (jj,), (0, 0, jj))
        for jj in range(1, jn)
    ]
    for copy in spread:
        copy.wait_recv()

    for i in range(2):
        for h in range(own_heads):
            for b in range(dn):
                source = factor[b, i, h].astype(f32)
                route = column(i, h, b)
                for e in range(E):
                    p = h * E + e
                    masked[
                        i,
                        p // 2,
                        b * seq_len : (b + 1) * seq_len,
                        (p % 2) * head_dim : (p % 2 + 1) * head_dim,
                    ] = jnp.where(route == e, source, 0.0).astype(bf16)
    couples = own_heads * E // 2
    step = min(width, 256)
    for n in range(0, width, step):
        added = jnp.zeros((dn * seq_len, step), f32)
        for c in range(couples):
            both = jnp.concatenate(
                [weight[0, 2 * c, n : n + step, :], weight[0, 2 * c + 1, n : n + step, :]], axis=1
            )
            added = added + across(masked[0, c], both)
        for r in range(dn * sources):
            term[r, :, n : n + step] = added[r * tok_rows : (r + 1) * tok_rows].astype(bf16)
    terms = []
    for slot, (dd, gg, jj) in enumerate(others):
        target = (
            lax.rem(d + dd, dn) * sources + lax.rem(g + gg, gn) * jn + lax.rem(j + jj, jn)
        )
        terms.append(
            send(term.at[target], term_in.at[d * sources + block], sem_term, (slot,), (dd, gg, jj))
        )
    term_in[d * sources + block] = term[d * sources + block]

    for i, out in enumerate((vg_out, og_out)):

        def one(c, carry, i=i, out=out):
            whole = jnp.dot(flat_t[i], masked[i, c], preferred_element_type=f32).astype(bf16)
            grads[i, 2 * c] = whole[:, :head_dim]
            grads[i, 2 * c + 1] = whole[:, head_dim:]
            pltpu.make_async_copy(
                grads.at[i, pl.ds(2 * c, 2)], out.at[pl.ds(2 * c, 2)], sem_grads.at[i, c]
            ).start()
            return carry

        lax.fori_loop(0, couples, one, 0)

    back_in[j] = back[j]
    for copy in returned:
        copy.wait_recv()
    for jj in range(jn):
        qg_out[jj] = back_in[jj, 0]
        kg_out[jj] = back_in[jj, 1]
    for copy in terms:
        copy.wait_recv()
    for b in range(dn):
        total_rows = term_in[b * sources].astype(f32)
        for s in range(1, sources):
            total_rows = total_rows + term_in[b * sources + s].astype(f32)
        tok_out[:, b * width : (b + 1) * width] = total_rows.astype(bf16)
    for i, out in enumerate((vg_out, og_out)):
        for c in range(couples):
            pltpu.make_async_copy(
                grads.at[i, pl.ds(2 * c, 2)], out.at[pl.ds(2 * c, 2)], sem_grads.at[i, c]
            ).wait()
    for copy in sent:
        copy.wait_send()


def fused(
    tokens,
    cotangent,
    queries,
    key_vectors,
    value_routes,
    output_routes,
    value_experts,
    output_experts,
):
    dn, gn, jn = lax.axis_size("dp"), lax.axis_size("head"), lax.axis_size("expert")
    expert_index = lax.axis_index("expert")
    _, tok_rows, model_width = tokens.shape
    width = model_width // dn
    _, query_rows, groups, head_dim = queries.shape
    seq_len = value_routes.shape[2]
    pairs_dev = value_experts.shape[0]
    own_heads = groups // jn
    sources = gn * jn
    bf16 = jnp.bfloat16

    routes = jnp.concatenate(
        [
            lax.dynamic_slice_in_dim(route[0, :, :, 0], expert_index * own_heads, own_heads, 0)
            for route in (value_routes, output_routes)
        ]
    )
    routes = jnp.pad(routes.T, ((0, 0), (0, 128 - 2 * own_heads)))

    def by_head(x):
        return x[0].transpose(1, 0, 2).reshape(jn, own_heads, query_rows, head_dim)

    vmem = pl.BlockSpec(memory_space=pltpu.VMEM)
    hbm = pl.BlockSpec(memory_space=pl.ANY)
    dma = pltpu.SemaphoreType.DMA
    head_block = (jn, own_heads, query_rows, head_dim)
    grad_shape = jax.ShapeDtypeStruct((pairs_dev, width, head_dim), bf16)
    tok_grads, query_grads, key_grads, value_grads, output_grads = pl.pallas_call(
        functools.partial(
            fused_kernel, (dn, gn, jn, own_heads, query_rows, tok_rows, width, head_dim)
        ),
        name="fused",
        out_shape=(
            jax.ShapeDtypeStruct((tok_rows, model_width), bf16),
            jax.ShapeDtypeStruct(head_block, bf16),
            jax.ShapeDtypeStruct(head_block, bf16),
            grad_shape,
            grad_shape,
        ),
        in_specs=[vmem] * 5 + [hbm] * 2,
        out_specs=(vmem, vmem, vmem, hbm, hbm),
        scratch_shapes=[
            pltpu.VMEM((sources, 2, dn, tok_rows, width), bf16),
            pltpu.VMEM((2, dn * seq_len, width), bf16),
            pltpu.VMEM((2, width, dn * seq_len), bf16),
            pltpu.VMEM((dn, seq_len, 128), jnp.int32),
            pltpu.VMEM((2, pairs_dev, width, head_dim), bf16),
            pltpu.VMEM((2, jn, own_heads, query_rows, head_dim), bf16),
            pltpu.VMEM((dn, 2, own_heads, seq_len, head_dim), bf16),
            pltpu.VMEM((dn, 2, own_heads, seq_len, head_dim), bf16),
            pltpu.VMEM((dn, 2, own_heads, seq_len, head_dim), bf16),
            pltpu.VMEM((2, pairs_dev // 2, dn * seq_len, 2 * head_dim), bf16),
            pltpu.VMEM((own_heads, seq_len, seq_len), bf16),
            pltpu.VMEM((jn, 2, own_heads, query_rows, head_dim), bf16),
            pltpu.VMEM((jn, 2, own_heads, query_rows, head_dim), bf16),
            pltpu.VMEM((dn * sources, tok_rows, width), bf16),
            pltpu.VMEM((dn * sources, tok_rows, width), bf16),
            pltpu.VMEM((2, pairs_dev, width, head_dim), bf16),
            dma((2,)),
            dma((5,)),
            dma((2, dn, 2)),
            dma((2, dn)),
            dma((2, gn)),
            dma((2, gn, jn)),
            dma((2, 2, jn)),
            dma((2, dn)),
            dma((2, dn)),
            dma((2, jn)),
            dma((2, dn * sources)),
            dma((2, pairs_dev // 2)),
        ],
        compiler_params=pltpu.CompilerParams(
            collective_id=0, has_side_effects=True, vmem_limit_bytes=60 * 1024 * 1024
        ),
    )(
        tokens[0],
        cotangent[0],
        by_head(queries),
        by_head(key_vectors),
        routes,
        value_experts,
        output_experts,
    )

    def by_row(x):
        return x.reshape(groups, query_rows, head_dim).transpose(1, 0, 2)[None]

    return tok_grads[None], by_row(query_grads), by_row(key_grads), value_grads, output_grads


def chosen(*args):
    groups, pairs_dev = args[2].shape[2], args[6].shape[0]
    dp_count, expert_count = lax.axis_size("dp"), lax.axis_size("expert")
    whole_heads = groups % expert_count == 0 and pairs_dev == groups // expert_count * E
    if whole_heads and args[0].shape[2] % (dp_count * 256) == 0 and args[2].shape[1] <= 64:
        return fused(*args)
    return local(*args)


def solution(mesh):
    return jax.shard_map(
        chosen,
        mesh=mesh,
        in_specs=(
            P("dp", ("head", "expert"), None),
            P("dp", ("head", "expert"), None),
            P("dp", "expert", "head", None),
            P("dp", "expert", "head", None),
            P("dp", "head", None, None),
            P("dp", "head", None, None),
            P(("head", "expert"), None, None),
            P(("head", "expert"), None, None),
        ),
        out_specs=(
            P("dp", ("head", "expert"), None),
            P("dp", "expert", "head", None),
            P("dp", "expert", "head", None),
            P(("head", "expert"), "dp", None),
            P(("head", "expert"), "dp", None),
        ),
        check_vma=False,
    )
```

```python
import functools

import jax
import jax.numpy as jnp
from jax import lax
from jax.experimental import pallas as pl
from jax.experimental.pallas import tpu as pltpu
from jax.sharding import PartitionSpec as P

E = 4
CAP = 3


def slot_rank(routes):
    onehot = (routes[..., None] == jnp.arange(E, dtype=jnp.int32)).astype(jnp.int32)
    before = jnp.cumsum(onehot, axis=-2) - onehot
    return jnp.sum(before * onehot, axis=-1)


def slot_table(routes):
    rank_of = slot_rank(routes)
    expert_hit = routes[..., None, None, :] == jnp.arange(E, dtype=jnp.int32)[:, None, None]
    place_hit = rank_of[..., None, None, :] == jnp.arange(CAP, dtype=jnp.int32)[:, None]
    return jnp.logical_and(expert_hit, place_hit).astype(jnp.bfloat16)


def local(
    tokens,
    cotangent,
    queries,
    key_vectors,
    value_routes,
    output_routes,
    value_experts,
    output_experts,
):
    head_count = lax.axis_size("head")
    expert_count = lax.axis_size("expert")
    sources = head_count * expert_count
    expert_index = lax.axis_index("expert")
    tok_rows = tokens.shape[1]
    model_width = tokens.shape[2]
    query_rows = queries.shape[1]
    groups = queries.shape[2]
    head_dim = queries.shape[3]
    seq_len = value_routes.shape[2]
    pairs_dev = value_experts.shape[0]
    slot_count = sources * CAP
    score_scale = head_dim ** (-0.5)
    value_local = value_routes[0, :, :, 0]
    output_local = output_routes[0, :, :, 0]

    def own_block(route_part):
        shaped = route_part.reshape(groups, head_count, expert_count, tok_rows)
        return lax.dynamic_index_in_dim(shaped, expert_index, 2, keepdims=False)

    own_pair = jnp.stack([own_block(value_local), own_block(output_local)])
    own_routes = lax.all_to_all(own_pair, "head", split_axis=2, concat_axis=1, tiled=True).reshape(
        2, groups * head_count, tok_rows
    )
    value_table = slot_table(own_routes[0]).reshape(
        head_count, expert_count, pairs_dev, CAP, tok_rows
    )

    def pair_rows(route_part, gathered):
        slot_map = slot_table(route_part.reshape(groups, sources, tok_rows))
        slot_map = jnp.moveaxis(slot_map, 2, 1).reshape(groups * E, sources, CAP, tok_rows)
        slot_map = lax.dynamic_slice_in_dim(slot_map, expert_index * pairs_dev, pairs_dev, 0)
        picked = jnp.einsum(
            "psmt,stw->psmw",
            slot_map,
            gathered.reshape(sources, tok_rows, model_width),
            preferred_element_type=jnp.float32,
        )
        return picked.astype(jnp.bfloat16).reshape(pairs_dev, slot_count, model_width)

    whole_tokens, whole_cotangent = (
        lax.all_gather(tokens[0], ("head", "expert"), axis=0, tiled=True),
        lax.all_gather(cotangent[0], ("head", "expert"), axis=0, tiled=True),
    )
    token_slots = pair_rows(value_local, whole_tokens)
    cotangent_slots = pair_rows(output_local, whole_cotangent)
    value_slots = jnp.einsum(
        "prw,pwk->prk", token_slots, value_experts, preferred_element_type=jnp.float32
    ).astype(jnp.bfloat16)
    upstream_slots = jnp.einsum(
        "prw,pwk->prk", cotangent_slots, output_experts, preferred_element_type=jnp.float32
    ).astype(jnp.bfloat16)
    query_start = expert_index * query_rows
    group_values, group_upstream, all_keys = (
        lax.all_gather(value_slots, "expert", axis=0, tiled=True),
        lax.all_gather(upstream_slots, "expert", axis=0, tiled=True),
        lax.all_gather(key_vectors[0], "expert", axis=0, tiled=True),
    )
    token_source = jnp.arange(seq_len, dtype=jnp.int32) // tok_rows
    head_base = jnp.arange(groups, dtype=jnp.int32)[:, None] * E
    value_rank = slot_rank(value_local.reshape(groups, sources, tok_rows)).reshape(groups, seq_len)
    value_index = (head_base + value_local) * slot_count + token_source * CAP + value_rank
    value_rows = group_values.reshape(-1, head_dim)[value_index]
    output_rank = slot_rank(output_local.reshape(groups, sources, tok_rows)).reshape(
        groups, seq_len
    )
    block_routes = lax.dynamic_slice_in_dim(output_local, query_start, query_rows, 1)
    block_rank = lax.dynamic_slice_in_dim(output_rank, query_start, query_rows, 1)
    block_source = lax.dynamic_slice_in_dim(token_source, query_start, query_rows, 0)
    upstream_index = (head_base + block_routes) * slot_count + block_source * CAP + block_rank
    upstream_rows = group_upstream.reshape(-1, head_dim)[upstream_index]
    query_own = queries[0]
    scores = (
        jnp.einsum("ihc,jhc->hij", query_own, all_keys, preferred_element_type=jnp.float32)
        * score_scale
    )
    query_pos = query_start + jnp.arange(query_rows, dtype=jnp.int32)
    causal = jnp.arange(seq_len, dtype=jnp.int32)[None, :] <= query_pos[:, None]
    row_top = jnp.max(jnp.where(causal, scores, -jnp.inf), axis=-1, keepdims=True)
    weights = jnp.where(causal, jnp.exp(scores - row_top), 0.0)
    probs_full = weights / jnp.sum(weights, axis=-1, keepdims=True)
    prob_half = probs_full.astype(jnp.bfloat16)
    outputs = jnp.einsum(
        "hij,hjc->hic", prob_half, value_rows, preferred_element_type=jnp.float32
    ).astype(jnp.bfloat16)
    row_delta = jnp.sum(outputs.astype(jnp.float32) * upstream_rows.astype(jnp.float32), axis=-1)
    prob_grads = jnp.einsum(
        "hic,hjc->hij", upstream_rows, value_rows, preferred_element_type=jnp.float32
    )
    score_grads = (probs_full * (prob_grads - row_delta[:, :, None])).astype(jnp.bfloat16)
    query_grads = (
        jnp.einsum("hij,jhc->ihc", score_grads, all_keys, preferred_element_type=jnp.float32)
        * score_scale
    ).astype(jnp.bfloat16)
    key_part = (
        jnp.einsum("hij,ihc->jhc", score_grads, query_own, preferred_element_type=jnp.float32)
        * score_scale
    )
    value_part = jnp.einsum(
        "hij,hic->jhc", prob_half, upstream_rows, preferred_element_type=jnp.float32
    )
    key_sum, value_sum = (
        lax.psum_scatter(key_part, "expert", scatter_dimension=0, tiled=True),
        lax.psum_scatter(value_part, "expert", scatter_dimension=0, tiled=True),
    )
    value_half = value_sum.astype(jnp.bfloat16)
    block_value_routes = lax.dynamic_slice_in_dim(value_local, query_start, query_rows, 1).reshape(
        groups, head_count, tok_rows
    )
    value_place = slot_table(block_value_routes)
    output_place = slot_table(block_routes.reshape(groups, head_count, tok_rows))
    value_send = jnp.einsum(
        "hsemt,sthc->hesmc",
        value_place,
        value_half.reshape(head_count, tok_rows, groups, head_dim),
        preferred_element_type=jnp.float32,
    )
    value_send = value_send.astype(jnp.bfloat16).reshape(groups * E, head_count * CAP, head_dim)
    output_send = jnp.einsum(
        "hsemt,hstc->hesmc",
        output_place,
        outputs.reshape(groups, head_count, tok_rows, head_dim),
        preferred_element_type=jnp.float32,
    )
    output_send = output_send.astype(jnp.bfloat16).reshape(groups * E, head_count * CAP, head_dim)
    output_slots, grad_slots = (
        lax.all_to_all(output_send, "expert", split_axis=0, concat_axis=1, tiled=True),
        lax.all_to_all(value_send, "expert", split_axis=0, concat_axis=1, tiled=True),
    )
    value_term = jnp.einsum(
        "prw,prk->pwk", token_slots, grad_slots, preferred_element_type=jnp.float32
    )
    output_term = jnp.einsum(
        "prw,prk->pwk", cotangent_slots, output_slots, preferred_element_type=jnp.float32
    )
    value_grads, output_grads = (
        lax.psum_scatter(
            value_term.astype(jnp.bfloat16), "dp", scatter_dimension=1, tiled=True
        ).astype(jnp.float32),
        lax.psum_scatter(
            output_term.astype(jnp.bfloat16), "dp", scatter_dimension=1, tiled=True
        ).astype(jnp.float32),
    )
    token_terms = jnp.einsum(
        "prk,pwk->prw", grad_slots, value_experts, preferred_element_type=jnp.float32
    ).astype(jnp.bfloat16)
    returned = lax.all_to_all(
        token_terms.reshape(pairs_dev, sources, CAP, model_width),
        ("head", "expert"),
        split_axis=1,
        concat_axis=0,
        tiled=True,
    )
    returned = returned.reshape(head_count, expert_count, pairs_dev, CAP, model_width)
    token_grads = jnp.einsum(
        "gjpmt,gjpmw->tw", value_table, returned, preferred_element_type=jnp.float32
    )
    return (
        token_grads.astype(jnp.bfloat16)[None],
        query_grads[None],
        key_sum.astype(jnp.bfloat16)[None],
        value_grads.astype(jnp.bfloat16),
        output_grads.astype(jnp.bfloat16),
    )


def fused_kernel(
    sizes,
    tok,
    cot,
    q_in,
    k_in,
    routes_in,
    value_hbm,
    output_hbm,
    tok_out,
    qg_out,
    kg_out,
    flat_out,
    masked_out,
    rows,
    flat,
    flat_t,
    by_heads,
    routes,
    weight,
    heads_in,
    part,
    part_in,
    factor,
    masked,
    score_keep,
    prob_keep,
    upstream_keep,
    back,
    back_in,
    term,
    term_in,
    sem_weight,
    sem_own,
    sem_rows,
    sem_routes,
    sem_line,
    sem_side,
    sem_heads,
    sem_part,
    sem_factor,
    sem_back,
    sem_term,
    sem_grads,
):
    dn, gn, jn, own_heads, query_rows, tok_rows, width, head_dim = sizes
    sources = gn * jn
    seq_len = sources * tok_rows
    scale = head_dim ** (-0.5)
    d, g, j = lax.axis_index("dp"), lax.axis_index("head"), lax.axis_index("expert")
    block = g * jn + j
    f32, bf16 = jnp.float32, jnp.bfloat16

    def at(dd, gg, jj):
        return {"dp": lax.rem(d + dd, dn), "head": lax.rem(g + gg, gn), "expert": lax.rem(j + jj, jn)}

    others = [
        (dd, gg, jj)
        for dd in range(dn)
        for gg in range(gn)
        for jj in range(jn)
        if (dd, gg, jj) != (0, 0, 0)
    ]
    sent = []

    def send(src, dst, sems, slot, where):
        copy = pltpu.make_async_remote_copy(
            src_ref=src,
            dst_ref=dst,
            send_sem=sems.at[(0,) + slot],
            recv_sem=sems.at[(1,) + slot],
            device_id=at(*where),
            device_id_type=pl.DeviceIdType.MESH,
        )
        copy.start()
        sent.append(copy)
        return copy

    def columns(index):
        return pl.ds(pl.multiple_of(index * width, 128), width)

    weights_on_way = [
        pltpu.make_async_copy(hbm.at[:, columns(d), :], weight.at[i], sem_weight.at[i])
        for i, hbm in enumerate((value_hbm, output_hbm))
    ]
    for copy in weights_on_way:
        copy.start()
    own = [
        pltpu.make_async_copy(tok.at[:, columns(d)], rows.at[block, 0, d], sem_own.at[0]),
        pltpu.make_async_copy(cot.at[:, columns(d)], rows.at[block, 1, d], sem_own.at[1]),
        pltpu.make_async_copy(routes_in, routes.at[d], sem_own.at[2]),
    ]
    for copy in own:
        copy.start()

    barrier = pltpu.get_barrier_semaphore()
    for where in others:
        pl.semaphore_signal(
            barrier, inc=1, device_id=at(*where), device_id_type=pl.DeviceIdType.MESH
        )
    pl.semaphore_wait(barrier, len(others))

    first, late, line, side = [[], []], [], [[], []], [[], []]
    for i in (1, 0):
        for dd in range(1, dn):
            target = columns(lax.rem(d + dd, dn))
            source = (tok, cot)[i]
            first[i].append(
                send(source.at[:, target], rows.at[block, i, d], sem_rows, (dd, i), (dd, 0, 0))
            )
        if i == 1:
            late = [
                send(routes_in, routes.at[d], sem_routes, (dd,), (dd, 0, 0))
                for dd in range(1, dn)
            ]
    for copy in own:
        copy.wait()
    for i in (1, 0):
        for copy in first[i]:
            copy.wait_recv()
        here = rows.at[block, i]
        for gg in range(1, gn):
            line[i].append(send(here, here, sem_line, (gg, i), (0, gg, 0)))
        for jj in range(1, jn):
            side[i].append(send(here, here, sem_side, (0, jj, i), (0, 0, jj)))
    for i, source in enumerate((q_in, k_in)):
        turned = jnp.transpose(source[...].astype(f32), (1, 0, 2)).astype(bf16)
        for jj in range(jn):
            by_heads[i, jj] = turned[jj * own_heads : (jj + 1) * own_heads]
        heads_in[i, j] = by_heads[i, j]
    swapped = []
    for jj in range(1, jn):
        peer = lax.rem(j + jj, jn)
        for i in range(2):
            swapped.append(
                send(by_heads.at[i, peer], heads_in.at[i, j], sem_heads, (i, jj), (0, 0, jj))
            )

    def forward(i):
        for gg in range(1, gn):
            line[i][gg - 1].wait_recv()
            came = rows.at[lax.rem(g + gn - gg, gn) * jn + j, i]
            for jj in range(1, jn):
                side[i].append(send(came, came, sem_side, (gg, jj, i), (0, 0, jj)))

    def flatten(i):
        for copy in side[i]:
            copy.wait_recv()
        for b in range(dn):
            piece = jnp.concatenate([rows[s, i, b].astype(f32) for s in range(sources)], axis=0)
            flat[i, b * seq_len : (b + 1) * seq_len, :] = piece.astype(bf16)

    def column(i, h, b):
        c = i * own_heads + h
        return jnp.broadcast_to(routes[b, :, c : c + 1], (seq_len, head_dim))

    def project(i):
        weights_on_way[i].wait()
        for h in range(own_heads):
            picked = [jnp.zeros((seq_len, head_dim), f32) for _ in range(dn)]
            for e in range(0, E, 2):
                p = h * E + e
                both = jnp.concatenate([weight[i, p], weight[i, p + 1]], axis=1)
                every = jnp.dot(flat[i], both, preferred_element_type=f32)
                for b in range(dn):
                    own_rows = every[b * seq_len : (b + 1) * seq_len]
                    route = column(i, h, b)
                    picked[b] = jnp.where(route == e, own_rows[:, :head_dim], picked[b])
                    picked[b] = jnp.where(route == e + 1, own_rows[:, head_dim:], picked[b])
            for b in range(dn):
                part[b, i, h] = picked[b].astype(bf16)
        return [
            send(
                part.at[lax.rem(d + dd, dn), i], part_in.at[dd, i], sem_part, (dd, i), (dd, 0, 0)
            )
            for dd in range(1, dn)
        ]

    forward(1)
    flatten(1)
    for copy in late:
        copy.wait_recv()
    upstream_on_way = project(1)
    forward(0)

    query_pos = lax.broadcasted_iota(jnp.int32, (seq_len, seq_len), 0)
    key_pos = lax.broadcasted_iota(jnp.int32, (seq_len, seq_len), 1)
    causal = key_pos <= query_pos

    def joined(i, h):
        return jnp.concatenate([heads_in[i, jj, h] for jj in range(jn)], axis=0)

    def total(i, h):
        whole = part[d, i, h].astype(f32)
        for dd in range(1, dn):
            whole = whole + part_in[dd, i, h].astype(f32)
        return whole.astype(bf16)

    def across(a, b):
        return lax.dot_general(a, b, (((1,), (1,)), ((), ())), preferred_element_type=f32)

    def over_rows(a, b):
        return lax.dot_general(a, b, (((0,), (0,)), ((), ())), preferred_element_type=f32)

    def mask(i):
        for h in range(own_heads):
            for b in range(dn):
                source = factor[b, i, h].astype(f32)
                route = column(i, h, b)
                for e in range(E):
                    p = h * E + e
                    masked[
                        i,
                        p // 2,
                        b * seq_len : (b + 1) * seq_len,
                        (p % 2) * head_dim : (p % 2 + 1) * head_dim,
                    ] = jnp.where(route == e, source, 0.0).astype(bf16)

    def spread(i):
        return [
            send(factor.at[d, i], factor.at[d, i], sem_factor, (dd, i), (dd, 0, 0))
            for dd in range(1, dn)
        ]

    for copy in swapped:
        copy.wait_recv()
    for h in range(own_heads):
        query, key = joined(0, h), joined(1, h)
        scores = across(query, key) * scale
        top = jnp.max(jnp.where(causal, scores, -jnp.inf), axis=-1, keepdims=True)
        soft = jnp.where(causal, jnp.exp(scores - top), 0.0)
        prob_keep[h] = soft / jnp.sum(soft, axis=-1, keepdims=True)
    for copy in upstream_on_way:
        copy.wait_recv()
    for h in range(own_heads):
        upstream_keep[h] = total(1, h)
        factor[d, 0, h] = over_rows(prob_keep[h].astype(bf16), upstream_keep[h]).astype(bf16)
    value_spread = spread(0)
    flatten(0)
    values_on_way = project(0)
    for copy in value_spread:
        copy.wait_recv()
    mask(0)
    couples = own_heads * E // 2
    step = min(width, 256)
    for n in range(0, width, step):
        added = jnp.zeros((dn * seq_len, step), f32)
        for c in range(couples):
            both = jnp.concatenate(
                [weight[0, 2 * c, n : n + step, :], weight[0, 2 * c + 1, n : n + step, :]], axis=1
            )
            added = added + across(masked[0, c], both)
        for r in range(dn * sources):
            term[r, :, n : n + step] = added[r * tok_rows : (r + 1) * tok_rows].astype(bf16)
    terms = []
    for slot, (dd, gg, jj) in enumerate(others):
        target = (
            lax.rem(d + dd, dn) * sources + lax.rem(g + gg, gn) * jn + lax.rem(j + jj, jn)
        )
        terms.append(
            send(term.at[target], term_in.at[d * sources + block], sem_term, (slot,), (dd, gg, jj))
        )
    term_in[d * sources + block] = term[d * sources + block]

    for copy in values_on_way:
        copy.wait_recv()
    for h in range(own_heads):
        value, upstream, probs = total(0, h), upstream_keep[h], prob_keep[h]
        output = jnp.dot(probs.astype(bf16), value, preferred_element_type=f32).astype(bf16)
        factor[d, 1, h] = output
        delta = jnp.sum(output.astype(f32) * upstream.astype(f32), axis=-1, keepdims=True)
        score_keep[h] = (probs * (across(upstream, value) - delta)).astype(bf16)
    output_spread = spread(1)
    for h in range(own_heads):
        query, key, score = joined(0, h), joined(1, h), score_keep[h]
        query_grad = (jnp.dot(score, key, preferred_element_type=f32) * scale).astype(bf16)
        key_grad = (over_rows(score, query) * scale).astype(bf16)
        for jj in range(jn):
            back[jj, 0, h] = query_grad[jj * query_rows : (jj + 1) * query_rows]
            back[jj, 1, h] = key_grad[jj * query_rows : (jj + 1) * query_rows]
    returned = [
        send(back.at[lax.rem(j + jj, jn)], back_in.at[j], sem_back, (jj,), (0, 0, jj))
        for jj in range(1, jn)
    ]
    for i in range(2):
        flat_t[i] = flat[i].T
    for copy in output_spread:
        copy.wait_recv()
    mask(1)
    outgoing = [
        pltpu.make_async_copy(flat_t, flat_out, sem_grads.at[0]),
        pltpu.make_async_copy(masked, masked_out, sem_grads.at[1]),
    ]
    for copy in outgoing:
        copy.start()

    back_in[j] = back[j]
    for copy in returned:
        copy.wait_recv()
    for jj in range(jn):
        qg_out[jj] = back_in[jj, 0]
        kg_out[jj] = back_in[jj, 1]
    for copy in terms:
        copy.wait_recv()
    for b in range(dn):
        total_rows = term_in[b * sources].astype(f32)
        for s in range(1, sources):
            total_rows = total_rows + term_in[b * sources + s].astype(f32)
        tok_out[:, b * width : (b + 1) * width] = total_rows.astype(bf16)
    for copy in outgoing:
        copy.wait()
    for copy in sent:
        copy.wait_send()


def finish_kernel(flat_t, masked, tok_in, qg_in, kg_in, tok_out, qg_out, kg_out, vg_out, og_out):
    @pl.when(pl.program_id(0) == 0)
    def _():
        tok_out[...] = tok_in[...]
        for source, out in ((qg_in, qg_out), (kg_in, kg_out)):
            out[...] = jnp.transpose(source[...].astype(jnp.float32), (1, 0, 2)).astype(out.dtype)

    half = masked.shape[-1] // 2
    for i, out in enumerate((vg_out, og_out)):
        whole = jnp.dot(flat_t[i], masked[i, 0], preferred_element_type=jnp.float32)
        out[0] = whole[:, :half].astype(out.dtype)
        out[1] = whole[:, half:].astype(out.dtype)


def fused(
    tokens,
    cotangent,
    queries,
    key_vectors,
    value_routes,
    output_routes,
    value_experts,
    output_experts,
):
    dn, gn, jn = lax.axis_size("dp"), lax.axis_size("head"), lax.axis_size("expert")
    expert_index = lax.axis_index("expert")
    _, tok_rows, model_width = tokens.shape
    width = model_width // dn
    _, query_rows, groups, head_dim = queries.shape
    seq_len = value_routes.shape[2]
    pairs_dev = value_experts.shape[0]
    own_heads = groups // jn
    sources = gn * jn
    bf16 = jnp.bfloat16

    routes = jnp.concatenate(
        [
            lax.dynamic_slice_in_dim(route[0, :, :, 0], expert_index * own_heads, own_heads, 0)
            for route in (value_routes, output_routes)
        ]
    )
    routes = jnp.pad(routes.T, ((0, 0), (0, 128 - 2 * own_heads)))

    vmem = pl.BlockSpec(memory_space=pltpu.VMEM)
    hbm = pl.BlockSpec(memory_space=pl.ANY)
    dma = pltpu.SemaphoreType.DMA
    head_block = (jn, own_heads, query_rows, head_dim)
    grad_shape = jax.ShapeDtypeStruct((pairs_dev, width, head_dim), bf16)
    couples, all_rows = pairs_dev // 2, dn * seq_len
    tok_grads, query_grads, key_grads, flat_t, masked = pl.pallas_call(
        functools.partial(
            fused_kernel, (dn, gn, jn, own_heads, query_rows, tok_rows, width, head_dim)
        ),
        name="fused",
        out_shape=(
            jax.ShapeDtypeStruct((tok_rows, model_width), bf16),
            jax.ShapeDtypeStruct(head_block, bf16),
            jax.ShapeDtypeStruct(head_block, bf16),
            jax.ShapeDtypeStruct((2, width, all_rows), bf16),
            jax.ShapeDtypeStruct((2, couples, all_rows, 2 * head_dim), bf16),
        ),
        in_specs=[vmem] * 5 + [hbm] * 2,
        out_specs=(vmem, vmem, vmem, hbm, hbm),
        scratch_shapes=[
            pltpu.VMEM((sources, 2, dn, tok_rows, width), bf16),
            pltpu.VMEM((2, dn * seq_len, width), bf16),
            pltpu.VMEM((2, width, dn * seq_len), bf16),
            pltpu.VMEM((2, jn, own_heads, query_rows, head_dim), bf16),
            pltpu.VMEM((dn, seq_len, 128), jnp.int32),
            pltpu.VMEM((2, pairs_dev, width, head_dim), bf16),
            pltpu.VMEM((2, jn, own_heads, query_rows, head_dim), bf16),
            pltpu.VMEM((dn, 2, own_heads, seq_len, head_dim), bf16),
            pltpu.VMEM((dn, 2, own_heads, seq_len, head_dim), bf16),
            pltpu.VMEM((dn, 2, own_heads, seq_len, head_dim), bf16),
            pltpu.VMEM((2, pairs_dev // 2, dn * seq_len, 2 * head_dim), bf16),
            pltpu.VMEM((own_heads, seq_len, seq_len), bf16),
            pltpu.VMEM((own_heads, seq_len, seq_len), jnp.float32),
            pltpu.VMEM((own_heads, seq_len, head_dim), bf16),
            pltpu.VMEM((jn, 2, own_heads, query_rows, head_dim), bf16),
            pltpu.VMEM((jn, 2, own_heads, query_rows, head_dim), bf16),
            pltpu.VMEM((dn * sources, tok_rows, width), bf16),
            pltpu.VMEM((dn * sources, tok_rows, width), bf16),
            dma((2,)),
            dma((3,)),
            dma((2, dn, 2)),
            dma((2, dn)),
            dma((2, gn, 2)),
            dma((2, gn, jn, 2)),
            dma((2, 2, jn)),
            dma((2, dn, 2)),
            dma((2, dn, 2)),
            dma((2, jn)),
            dma((2, dn * sources)),
            dma((2,)),
        ],
        compiler_params=pltpu.CompilerParams(
            collective_id=0, has_side_effects=True, vmem_limit_bytes=60 * 1024 * 1024
        ),
    )(
        tokens[0],
        cotangent[0],
        queries[0],
        key_vectors[0],
        routes,
        value_experts,
        output_experts,
    )

    def fixed(shape):
        return pl.BlockSpec(shape, lambda c: (0,) * len(shape))

    by_head = (groups, query_rows, head_dim)
    by_row = (query_rows, groups, head_dim)
    grad_block = pl.BlockSpec((2, width, head_dim), lambda c: (c, 0, 0))
    row_shape = jax.ShapeDtypeStruct(by_row, bf16)
    tok_grads, query_grads, key_grads, value_grads, output_grads = pl.pallas_call(
        finish_kernel,
        name="finish",
        grid=(couples,),
        out_shape=(
            jax.ShapeDtypeStruct((tok_rows, model_width), bf16),
            row_shape,
            row_shape,
            grad_shape,
            grad_shape,
        ),
        in_specs=[
            fixed((2, width, all_rows)),
            pl.BlockSpec((2, 1, all_rows, 2 * head_dim), lambda c: (0, c, 0, 0)),
            fixed((tok_rows, model_width)),
            fixed(by_head),
            fixed(by_head),
        ],
        out_specs=(
            fixed((tok_rows, model_width)),
            fixed(by_row),
            fixed(by_row),
            grad_block,
            grad_block,
        ),
        compiler_params=pltpu.CompilerParams(vmem_limit_bytes=60 * 1024 * 1024),
    )(flat_t, masked, tok_grads, query_grads.reshape(by_head), key_grads.reshape(by_head))
    return tok_grads[None], query_grads[None], key_grads[None], value_grads, output_grads


def chosen(*args):
    groups, pairs_dev = args[2].shape[2], args[6].shape[0]
    dp_count, expert_count = lax.axis_size("dp"), lax.axis_size("expert")
    whole_heads = groups % expert_count == 0 and pairs_dev == groups // expert_count * E
    if whole_heads and args[0].shape[2] % (dp_count * 256) == 0 and args[2].shape[1] <= 64:
        return fused(*args)
    return local(*args)


def solution(mesh):
    return jax.shard_map(
        chosen,
        mesh=mesh,
        in_specs=(
            P("dp", ("head", "expert"), None),
            P("dp", ("head", "expert"), None),
            P("dp", "expert", "head", None),
            P("dp", "expert", "head", None),
            P("dp", "head", None, None),
            P("dp", "head", None, None),
            P(("head", "expert"), None, None),
            P(("head", "expert"), None, None),
        ),
        out_specs=(
            P("dp", ("head", "expert"), None),
            P("dp", "expert", "head", None),
            P("dp", "expert", "head", None),
            P(("head", "expert"), "dp", None),
            P(("head", "expert"), "dp", None),
        ),
        check_vma=False,
    )
```
